32 devices in a mesh: dp: 16 (over z, x, core), tensor: 2 (over y).
Axes of the slice: x: 2, y: 2, z: 4, core: 2. Of those that a mesh axis runs over, the one named last changes fastest.
Arguments:
- tokens: bfloat16 [32768, 512], P('dp'), may hold values from -6 to 6
- seq_lengths: int32 [32], P('dp'), may hold values from 1024 to 1024, as said below
- packed_slot: int32 [32768], P('dp'), may hold values from 0 to 32767, as said below
- out_grad: bfloat16 [32768, 512], P('dp'), may hold values from -6 to 6
- qkv_weight: bfloat16 [3, 512, 512], P(None, None, 'tensor'), may hold values from -0.25 to 0.25
- out_weight: bfloat16 [512, 512], P('tensor'), may hold values from -2 to 2
- up_weight: bfloat16 [512, 2048], P(None, 'tensor'), may hold values from -0.25 to 0.25
- down_weight: bfloat16 [2048, 512], P('tensor'), may hold values from -0.125 to 0.125
- gain_first: float32 [512], replicated, may hold values from 0.1 to 1.9
- shift_first: float32 [512], replicated, may hold values from -0.6 to 0.6
- gain_second: float32 [512], replicated, may hold values from 0.1 to 1.9
- shift_second: float32 [512], replicated, may hold values from -0.6 to 0.6
- up_bias: float32 [2048], P('tensor'), may hold values from -12 to 12
Outputs:
- layer_out: bfloat16 [32768, 512], P('dp')
- grad_input: bfloat16 [32768, 512], P('dp')
- grad_qkv: float32 [3, 512, 512], P(None, None, 'tensor')
- grad_outproj: float32 [512, 512], P('tensor')
- grad_up: float32 [512, 2048], P(None, 'tensor')
- grad_down: float32 [2048, 512], P('tensor')
- grad_gain_first: float32 [512], replicated
- grad_shift_first: float32 [512], replicated
- grad_gain_second: float32 [512], replicated
- grad_shift_second: float32 [512], replicated
- grad_up_bias: float32 [2048], P('tensor')
The draws below stay inside these ranges and needn't reach their ends.
Inputs may be any that keep to these rules, and one draw needn't show every extreme that they name: Each pair seq_lengths[2b], seq_lengths[2b+1] sums to 2048; every length is a multiple of 64; some pair is (1024, 1024). packed_slot is a permutation of the rows; of the 2048 rows of one index of dp, exactly 128 have packed_slot // 2048 equal to each index of dp.
All inputs are finite; a program needn't handle non-finite values.
Results may differ from the reference program's by a relative error of at most 0.015.
Values may be sent and summed in bfloat16 or wider, within the bound.
No kernel may reach another device: no remote copies, remote signals or barrier semaphores. Data moves between devices by JAX's collectives and lax.ppermute only.
A program may use at most 192 MiB of HBM per device.

```python
import jax
import jax.numpy as jnp
from jax import lax

D = 512
HD = 64
FF = 2048
BLK = 64
MIN_LEN = 1024
TOK_DEV = 2048
TOKENS = 32768
SEQS = 32
N_DP = 16
N_TENSOR = 2


def draw_seq_lengths(key, part):
    ndev = SEQS // 2
    span = (TOK_DEV - 2 * MIN_LEN) // BLK + 1
    first = MIN_LEN + BLK * jax.random.randint(jax.random.fold_in(key, 11), (ndev,), 0, span)
    chosen = jax.random.randint(jax.random.fold_in(key, 12), (), 0, ndev)
    first = jnp.where(jnp.arange(ndev) == chosen, TOK_DEV - MIN_LEN, first)
    return jnp.stack([first, TOK_DEV - first], axis=1).reshape(SEQS).astype(jnp.int32)


def draw_packed_slot(key, part):
    ndev = TOKENS // TOK_DEV
    slot = TOK_DEV // ndev
    base = jnp.tile(jnp.repeat(jnp.arange(ndev, dtype=jnp.int32), slot)[None, :], (ndev, 1))
    target = jax.random.permutation(jax.random.fold_in(key, 21), base, axis=1, independent=True)
    sorter = jnp.argsort(target, axis=1, stable=True)
    inverse = jnp.argsort(sorter, axis=1, stable=True)
    rank = (inverse % slot).astype(jnp.int32)
    incoming = jnp.arange(ndev, dtype=jnp.int32)[:, None] * slot + rank
    order = jnp.tile(jnp.arange(TOK_DEV, dtype=jnp.int32)[None, :], (ndev, 1))
    shuffle = jax.random.permutation(jax.random.fold_in(key, 22), order, axis=1, independent=True)
    place = target * TOK_DEV + shuffle[target, incoming]
    return place.reshape(TOKENS).astype(jnp.int32)


def levels(stream_key, extent, shards, least, high):
    factor_of, own = 1.0, jax.random.fold_in(stream_key, 6)
    for axis_at, blocks in shards:
        heights = jnp.exp(jax.random.uniform(jax.random.fold_in(own, axis_at), (blocks,), jnp.float32, least / len(shards), high / len(shards)))
        factor_of = factor_of * jnp.repeat(heights, extent[axis_at] // blocks).reshape([-1 if axis == axis_at else 1 for axis in range(len(extent))])
    return factor_of


def normal_values(rng, extent, scale, limit, pieces=(), kind=jnp.bfloat16):
    entries = scale * jax.random.normal(rng, extent, jnp.float32)
    if pieces:
        entries = entries * levels(rng, extent, pieces, -0.22, 0.18)
    return jnp.clip(entries, -limit, limit).astype(kind)


def setup_inputs(seed: int = 0) -> dict:
    key_list = jax.random.split(jax.random.key(seed), 14)
    tokens = normal_values(key_list[0], (TOKENS, D), 1.0, 6.0, ((0, 16),))
    seq_lengths = draw_seq_lengths(jax.random.fold_in(key_list[13], 71), 0)
    packed_slot = draw_packed_slot(jax.random.fold_in(key_list[13], 71), 0)
    out_grad = normal_values(key_list[3], (TOKENS, D), 1.0, 6.0, ((0, 16),))
    qkv_weight = normal_values(key_list[4], (3, D, D), D ** -0.5, 0.25, ((2, 2),))
    out_weight = normal_values(key_list[5], (D, D), 8 ** -0.5, 2.0, ((0, 2),))
    up_weight = normal_values(key_list[6], (D, FF), D ** -0.5, 0.25, ((1, 2),))
    down_weight = normal_values(key_list[7], (FF, D), FF ** -0.5, 0.125, ((0, 2),))
    gain_first = jnp.clip(1.0 + 0.18 * jax.random.normal(key_list[8], (D,), jnp.float32), 0.1, 1.9)
    shift_first = normal_values(key_list[9], (D,), 0.1, 0.6, (), jnp.float32)
    gain_second = jnp.clip(1.0 + 0.18 * jax.random.normal(key_list[10], (D,), jnp.float32), 0.1, 1.9)
    shift_second = normal_values(key_list[11], (D,), 0.1, 0.6, (), jnp.float32)
    up_bias = normal_values(key_list[12], (FF,), 3.0, 12.0, ((0, 2),), jnp.float32)
    return {"tokens": tokens, "seq_lengths": seq_lengths, "packed_slot": packed_slot, "out_grad": out_grad, "qkv_weight": qkv_weight, "out_weight": out_weight, "up_weight": up_weight, "down_weight": down_weight, "gain_first": gain_first, "shift_first": shift_first, "gain_second": gain_second, "shift_second": shift_second, "up_bias": up_bias}


@jax.custom_vjp
def low(v):
    return lax.optimization_barrier(v.astype(jnp.bfloat16)).astype(jnp.float32)

@jax.custom_vjp
def low_back(v):
    return v

def low_keep(v):
    return (low(v), None)

def low_pass(kept, grad):
    return (grad,)

def back_keep(v):
    return (v, None)

def back_low(kept, grad):
    return (low(grad),)
low.defvjp(low_keep, low_pass)
low_back.defvjp(back_keep, back_low)

def layer_norm(value, gain, shift):
    mean = lax.optimization_barrier(jnp.mean(value, axis=-1, keepdims=True))
    cent = value - mean
    var = lax.optimization_barrier(jnp.mean(cent * cent, axis=-1, keepdims=True))
    return cent * lax.rsqrt(var + 1e-05) * gain + shift

def feature(value):
    return jnp.where(value > 0, value + 1.0, jnp.exp(jnp.minimum(value, 0.0)))

def linear_attention(q_feat, k_feat, v_feat, stretch_seq):
    best = lax.Precision.HIGHEST
    nblk = q_feat.shape[0] // BLK
    query = q_feat.reshape(nblk, BLK, -1, HD)
    keys = k_feat.reshape(nblk, BLK, -1, HD)
    values = v_feat.reshape(nblk, BLK, -1, HD)
    outer = jnp.einsum('cjhe,cjhf->chef', keys, values, precision=best)
    ksum = lax.optimization_barrier(jnp.sum(keys, axis=1))
    index = jnp.arange(nblk)
    mixing = ((index[None, :] < index[:, None]) & (stretch_seq[None, :] == stretch_seq[:, None])).astype(jnp.float32)
    state = jnp.einsum('cd,dhef->chef', mixing, outer, precision=best)
    zsum = jnp.einsum('cd,dhe->che', mixing, ksum, precision=best)
    scores = jnp.einsum('cihe,cjhe->chij', query, keys, precision=best)
    lower = (jnp.arange(BLK)[None, :] <= jnp.arange(BLK)[:, None]).astype(jnp.float32)
    scores = scores * lower
    numer = jnp.einsum('cihe,chef->cihf', query, state, precision=best)
    numer = numer + jnp.einsum('chij,cjhf->cihf', scores, values, precision=best)
    denom = jnp.einsum('cihe,che->cih', query, zsum, precision=best)
    denom = denom + jnp.transpose(lax.optimization_barrier(jnp.sum(scores, axis=-1)), (0, 2, 1)) + 1e-06
    result = numer / denom[..., None]
    return result.reshape(nblk * BLK, -1)

def block_forward(block_x, lens, params):
    best = lax.Precision.HIGHEST
    qkv_weight, out_weight, up_weight, down_weight, gain_first, shift_first, gain_second, shift_second, up_bias = params
    nblk = block_x.shape[0] // BLK
    stretch_seq = (jnp.arange(nblk) * BLK >= lens[0]).astype(jnp.int32)
    width = D // N_TENSOR
    units = FF // N_TENSOR
    first = low(layer_norm(block_x, gain_first, shift_first))
    attn = jnp.zeros(block_x.shape, jnp.float32)
    for group in range(N_TENSOR):
        own = low_back(first)
        weight = qkv_weight[:, :, group * width:(group + 1) * width]
        raw = low_back(jnp.einsum('td,jdc->jtc', own, weight, precision=best))
        q_feat = low(feature(raw[0]))
        k_feat = low(feature(raw[1]))
        v_feat = low(raw[2])
        heads = low(linear_attention(q_feat, k_feat, v_feat, stretch_seq))
        attn = attn + low(jnp.dot(heads, out_weight[group * width:(group + 1) * width], precision=best))
    middle = block_x + low_back(attn)
    second = low(layer_norm(middle, gain_second, shift_second))
    ffn = jnp.zeros(block_x.shape, jnp.float32)
    for group in range(N_TENSOR):
        own = low_back(second)
        lifted = jnp.dot(own, up_weight[:, group * units:(group + 1) * units], precision=best) + up_bias[group * units:(group + 1) * units]
        hidden = low_back(lifted)
        active = low(jax.nn.silu(hidden))
        ffn = ffn + low(jnp.dot(active, down_weight[group * units:(group + 1) * units], precision=best))
    return middle + low_back(ffn)

def reference(tokens, seq_lengths, packed_slot, out_grad, qkv_weight, out_weight, up_weight, down_weight, gain_first, shift_first, gain_second, shift_second, up_bias):
    packed_x = jnp.zeros((TOKENS, D), jnp.float32).at[packed_slot].set(tokens.astype(jnp.float32))
    packed_g = jnp.zeros((TOKENS, D), jnp.float32).at[packed_slot].set(out_grad.astype(jnp.float32))
    params = (qkv_weight.astype(jnp.float32), out_weight.astype(jnp.float32), up_weight.astype(jnp.float32), down_weight.astype(jnp.float32), gain_first.astype(jnp.float32), shift_first.astype(jnp.float32), gain_second.astype(jnp.float32), shift_second.astype(jnp.float32), up_bias.astype(jnp.float32))
    lens = seq_lengths.reshape(N_DP, 2)

    def whole(values, weights):
        blocks = values.reshape(N_DP, TOK_DEV, D)
        runner = jax.checkpoint(lambda xb, lb: block_forward(xb, lb, weights))
        outs = lax.map(lambda pair: runner(pair[0], pair[1]), (blocks, lens))
        return outs.reshape(TOKENS, D)
    result, pull = jax.vjp(whole, packed_x, params)
    grad_x, grads = pull(packed_g)
    layer_out = result[packed_slot].astype(jnp.bfloat16)
    grad_input = grad_x[packed_slot].astype(jnp.bfloat16)
    return (layer_out, grad_input, grads[0], grads[1], grads[2], grads[3], grads[4], grads[5], grads[6], grads[7], grads[8])
```

```python
import functools

import jax
import jax.numpy as jnp
from jax import lax
from jax.experimental import pallas as pl
from jax.experimental.pallas import tpu as pltpu
from jax.sharding import PartitionSpec as P

HD = 64
BLK = 64
TILE = 256
HEADER = 8
EPS = 1e-05
BF16 = jnp.bfloat16
F32 = jnp.float32
VMEM_LIMIT = 56 * 1024 * 1024


def dot(a, b):
    return jnp.dot(a, b, preferred_element_type=F32)


def dot_t(a, b):
    return lax.dot_general(a, b, (((1,), (1,)), ((), ())), preferred_element_type=F32)


def iota(shape, dim):
    return lax.broadcasted_iota(jnp.int32, shape, dim)


def one_hot(match):
    return jnp.where(match, 1.0, 0.0).astype(BF16)


def call(body, outs, scratch=(), in_specs=None, flops=0, moved=0, trans=0, limit=VMEM_LIMIT):
    return pl.pallas_call(
        body,
        out_shape=outs,
        in_specs=in_specs,
        scratch_shapes=list(scratch),
        compiler_params=pltpu.CompilerParams(vmem_limit_bytes=limit),
        cost_estimate=pl.CostEstimate(flops=flops, bytes_accessed=moved, transcendentals=trans),
    )


def shaped(shape, kind):
    return jax.ShapeDtypeStruct(shape, kind)


SMEM = pl.BlockSpec(memory_space=pltpu.SMEM)
VMEM = pl.BlockSpec(memory_space=pltpu.VMEM)


def send_tokens_body(ids_ref, slot_ref, tok_ref, out_ref, place_ref):
    own_plane = ids_ref[1]
    rows = tok_ref.shape[0]
    count, slot = out_ref.shape[0], out_ref.shape[1] - HEADER
    half = out_ref.shape[2]
    slots = slot_ref[...]
    block = slots // rows
    local = slots - block * rows
    member = one_hot(iota((count, rows), 0) == block)
    before = one_hot(iota((TILE, TILE), 0) < iota((TILE, TILE), 1))
    carry = jnp.zeros((count, 1), F32)
    ranks = []
    for at in range(0, rows, TILE):
        seg = member[:, at : at + TILE]
        inside = dot(seg, before) + carry
        segf = seg.astype(F32)
        ranks.append(jnp.sum(segf * inside, axis=0, keepdims=True))
        carry = carry + jnp.sum(segf, axis=1, keepdims=True)
    rank = jnp.concatenate(ranks, axis=1).astype(jnp.int32)
    pair = block // 2
    place = pair * slot + rank + jnp.where(block - 2 * pair == own_plane, 0, rows // 2)
    place_ref[...] = place
    high = local // 128
    low = local - high * 128
    line = iota((16, rows), 0)
    marks = jnp.where(line == 0, high, jnp.where(line == 1, low, 0)).astype(F32).astype(BF16)
    per = TILE // slot

    def step(t, _):
        pick = one_hot(iota((TILE, rows), 0) + t * TILE == place)
        moved = dot(pick, tok_ref[...]).astype(BF16)
        head = dot_t(marks, pick)[:HEADER].astype(BF16)
        for j in range(per):
            for side in range(2):
                to = 2 * (t * per + j) + side
                out_ref[to, 0:slot, :] = moved[
                    j * slot : (j + 1) * slot, side * half : (side + 1) * half
                ]
                out_ref[to, slot : slot + HEADER, :] = head
        return 0

    lax.fori_loop(0, rows // 2 // TILE, step, 0)


def send_grads_body(place_ref, tok_ref, out_ref):
    rows = tok_ref.shape[0]
    slot, half = out_ref.shape[1], out_ref.shape[2]
    per = TILE // slot
    place = place_ref[...]

    def step(t, _):
        pick = one_hot(iota((TILE, rows), 0) + t * TILE == place)
        moved = dot(pick, tok_ref[...]).astype(BF16)
        for j in range(per):
            for side in range(2):
                out_ref[2 * (t * per + j) + side] = moved[
                    j * slot : (j + 1) * slot, side * half : (side + 1) * half
                ]
        return 0

    lax.fori_loop(0, rows // 2 // TILE, step, 0)


def received(core, pick, mine, other):
    a = dot(pick, mine)
    b = dot(pick, other)
    first = core == 0
    return jnp.concatenate([jnp.where(first, a, b), jnp.where(first, b, a)], axis=1)


def norm_parts(value):
    mean = jnp.mean(value, axis=-1, keepdims=True)
    cent = value - mean
    var = jnp.mean(cent * cent, axis=-1, keepdims=True)
    inv = lax.rsqrt(var + EPS)
    return cent * inv, inv


def norm_back(grad, xhat, inv, gain):
    e = grad * gain
    m1 = jnp.mean(e, axis=-1, keepdims=True)
    m2 = jnp.mean(e * xhat, axis=-1, keepdims=True)
    return inv * (e - m1 - xhat * m2)


def feature(value):
    return jnp.where(value > 0, value + 1.0, jnp.exp(jnp.minimum(value, 0.0)))


def head_mask(kind):
    n = 4 * HD
    return (iota((n, n), 0) // HD == iota((n, n), 1) // HD).astype(F32).astype(kind)


def spread(x, mask):
    return jnp.concatenate([x, x, x, x], axis=0) * mask


def attend_body(
    ids_ref, spos_ref, mine_ref, other_ref, wown_ref, wa_ref, wb_ref, oown_ref, oa_ref, ob_ref,
    gain_ref, shift_ref,
    x_ref, h1_ref, qkv_ref, o_ref, rden_ref, s_ref, z_ref, m_ref,
    wg_ref, og_ref, state_ref, zsum_ref,
):
    core = ids_ref[0]
    count, slot, half = mine_ref.shape[0], mine_ref.shape[1] - HEADER, mine_ref.shape[2]
    rows = count * slot
    seq = rows // 2
    width = 4 * HD
    for j in range(3):
        wg_ref[j, :, 0 : width // 2] = wa_ref[j]
        wg_ref[j, :, width // 2 : width] = wb_ref[j]
    og_ref[0 : width // 2, :] = oa_ref[...]
    og_ref[width // 2 : width, :] = ob_ref[...]
    spos = spos_ref[...]
    gain, shift = gain_ref[...], shift_ref[...]

    def project(t, _):
        at = pl.multiple_of(t * TILE, TILE)
        pick = one_hot(iota((TILE, rows), 0) + core * seq + t * TILE == spos)
        mine = mine_ref[:, 0:slot, :].reshape(rows, half)
        other = other_ref[:, 0:slot, :].reshape(rows, half)
        x = received(core, pick, mine, other)
        x_ref[pl.ds(at, TILE), :] = x.astype(BF16)
        xhat, _inv = norm_parts(x)
        h1 = (xhat * gain + shift).astype(BF16)
        h1_ref[pl.ds(at, TILE), :] = h1
        for g in range(2):
            for j in range(3):
                w = wown_ref[j] if g == 0 else wg_ref[j]
                u = dot(h1, w)
                if j < 2:
                    u = feature(u)
                qkv_ref[j, g, pl.ds(at, TILE), :] = u.astype(BF16)
        return 0

    lax.fori_loop(0, seq // TILE, project, 0)

    state_ref[...] = jnp.zeros_like(state_ref)
    zsum_ref[...] = jnp.zeros_like(zsum_ref)
    maskf = head_mask(F32)
    mask = maskf.astype(BF16)
    lower = iota((BLK, width), 1) % BLK <= iota((BLK, width), 0)

    def chunk(c, _):
        at = pl.multiple_of(c * BLK, BLK)
        for g in range(2):
            q = qkv_ref[0, g, pl.ds(at, BLK), :]
            k = qkv_ref[1, g, pl.ds(at, BLK), :]
            v = qkv_ref[2, g, pl.ds(at, BLK), :]
            state = state_ref[g]
            low = state.astype(BF16)
            s_ref[g, c] = low
            z = zsum_ref[g]
            z_ref[g, c] = z
            scores = jnp.where(lower, dot_t(q, spread(k, mask)), 0.0)
            num = dot(q, low) + dot(scores.astype(BF16), spread(v, mask))
            den = dot((scores + q.astype(F32) * z[0:1]).astype(BF16), mask) + 1e-06
            rden = 1.0 / den
            rden_ref[g, pl.ds(at, BLK), :] = rden
            o_ref[g, pl.ds(at, BLK), :] = (num * rden).astype(BF16)
            state_ref[g] = state + dot(k.T, v) * maskf
            zsum_ref[g] = z + jnp.sum(k.astype(F32), axis=0, keepdims=True)
        return 0

    lax.fori_loop(0, seq // BLK, chunk, 0, unroll=2)

    def output(t, _):
        at = pl.multiple_of(t * TILE, TILE)
        att = dot(o_ref[0, pl.ds(at, TILE), :], oown_ref[...])
        att = att + dot(o_ref[1, pl.ds(at, TILE), :], og_ref[...])
        m_ref[pl.ds(at, TILE), :] = x_ref[pl.ds(at, TILE), :].astype(F32) + att
        return 0

    lax.fori_loop(0, seq // TILE, output, 0)


def ffn_body(
    ids_ref, spos_ref, mine_ref, other_ref, m_ref, uown_ref, ua_ref, ub_ref,
    down_ref, da_ref, db_ref, bias_ref, gain_ref, shift_ref,
    keep_ref, send_ref, dm_ref, grad_ref, vec_ref, bvec_ref,
    gpt_ref, h2t_ref, rl_ref, du_ref,
):
    core = ids_ref[0]
    count, slot, half = mine_ref.shape
    rows = count * slot
    seq = rows // 2
    unit = ua_ref.shape[1]
    spos = spos_ref[...]
    gain, shift = gain_ref[...], shift_ref[...]
    vec_ref[...] = jnp.zeros_like(vec_ref)
    bvec_ref[...] = jnp.zeros_like(bvec_ref)

    def up_piece(j):
        if j < 2:
            return uown_ref[:, j * unit : (j + 1) * unit]
        return ua_ref[...] if j == 2 else ub_ref[...]

    def down_piece(j):
        if j < 2:
            return down_ref[j * unit : (j + 1) * unit, :]
        return da_ref[...] if j == 2 else db_ref[...]

    def tile(t, _):
        at = pl.multiple_of(t * TILE, TILE)
        pick = one_hot(iota((TILE, rows), 0) + core * seq + t * TILE == spos)
        gpf = received(core, pick, mine_ref[...].reshape(rows, half), other_ref[...].reshape(rows, half))
        gp = gpf.astype(BF16)
        m = m_ref[pl.ds(at, TILE), :]
        xhat, inv = norm_parts(m)
        h2 = (xhat * gain + shift).astype(BF16)
        gpt_ref[:, pl.ds(at, TILE)] = gp.T
        h2t_ref[:, pl.ds(at, TILE)] = h2.T
        f = jnp.zeros((TILE, m.shape[1]), F32)
        dh2 = jnp.zeros((TILE, m.shape[1]), F32)
        for j in range(4):
            up, down = up_piece(j), down_piece(j)
            u = dot(h2, up) + bias_ref[j : j + 1, :]
            sig = jax.nn.sigmoid(u)
            rl = (u * sig).astype(BF16)
            rl_ref[j, pl.ds(at, TILE), :] = rl
            f = f + dot(rl, down)
            du = dot_t(gp, down) * (sig * (1.0 + u * (1.0 - sig)))
            dul = du.astype(BF16)
            du_ref[j, pl.ds(at, TILE), :] = dul
            bvec_ref[j : j + 1, :] += jnp.sum(dul.astype(F32), axis=0, keepdims=True)
            dh2 = dh2 + dot_t(dul, up)
        out = (m + f).astype(BF16)
        left, right = out[:, :half], out[:, half:]
        first = core == 0
        keep_ref[pl.ds(at, TILE), :] = jnp.where(first, left, right)
        send_ref[pl.ds(at, TILE), :] = jnp.where(first, right, left)
        vec_ref[0:1, :] += jnp.sum(dh2 * xhat, axis=0, keepdims=True)
        vec_ref[1:2, :] += jnp.sum(dh2, axis=0, keepdims=True)
        dm_ref[pl.ds(at, TILE), :] = gpf + norm_back(dh2, xhat, inv, gain)
        return 0

    lax.fori_loop(0, seq // TILE, tile, 0)

    for j in range(4):
        where = (j ^ core) if j < 2 else j - 2
        side = 0 if j < 2 else 1
        grad_ref[where, side, 0] = dot(h2t_ref[...], du_ref[j]).astype(BF16)
        grad_ref[where, side, 1] = dot(gpt_ref[...], rl_ref[j]).astype(BF16)


def attend_back_body(
    ids_ref, dm_ref, oown_ref, oa_ref, ob_ref, qkv_ref, o_ref, rden_ref, s_ref, z_ref,
    h1_ref, x_ref, wown_ref, wa_ref, wb_ref, gain_ref,
    keep_ref, send_ref, grad_ref, vec_ref,
    wg_ref, og_ref, dmt_ref, h1t_ref, dn_ref, w_ref, dr_ref, state_ref, zsum_ref,
):
    core = ids_ref[0]
    seq, d = dm_ref.shape
    width = 4 * HD
    part = width // 2
    half = keep_ref.shape[1]
    for j in range(3):
        wg_ref[j, :, 0:part] = wa_ref[j]
        wg_ref[j, :, part:width] = wb_ref[j]
    og_ref[0:part, :] = oa_ref[...]
    og_ref[part:width, :] = ob_ref[...]
    vec_ref[...] = jnp.zeros_like(vec_ref)

    def start(t, _):
        at = pl.multiple_of(t * TILE, TILE)
        dml = dm_ref[pl.ds(at, TILE), :].astype(BF16)
        dmt_ref[:, pl.ds(at, TILE)] = dml.T
        h1t_ref[:, pl.ds(at, TILE)] = h1_ref[pl.ds(at, TILE), :].T
        for g in range(2):
            do = dot_t(dml, oown_ref[...] if g == 0 else og_ref[...])
            dn = do * rden_ref[g, pl.ds(at, TILE), :]
            dn_ref[g, pl.ds(at, TILE), :] = dn.astype(BF16)
            w_ref[g, pl.ds(at, TILE), :] = (
                -dn * o_ref[g, pl.ds(at, TILE), :].astype(F32)
            ).astype(BF16)
        return 0

    lax.fori_loop(0, seq // TILE, start, 0)

    state_ref[...] = jnp.zeros_like(state_ref)
    zsum_ref[...] = jnp.zeros_like(zsum_ref)
    maskf = head_mask(F32)
    mask = maskf.astype(BF16)
    ones = jnp.ones((16, width), BF16)
    lower = iota((BLK, width), 1) % BLK <= iota((BLK, width), 0)
    upper = iota((BLK, width), 1) % BLK >= iota((BLK, width), 0)
    nblk = seq // BLK

    def chunk(step, _):
        c = nblk - 1 - step
        at = pl.multiple_of(c * BLK, BLK)
        for g in range(2):
            q = qkv_ref[0, g, pl.ds(at, BLK), :]
            k = qkv_ref[1, g, pl.ds(at, BLK), :]
            v = qkv_ref[2, g, pl.ds(at, BLK), :]
            dn = dn_ref[g, pl.ds(at, BLK), :]
            w = w_ref[g, pl.ds(at, BLK), :]
            state = state_ref[g]
            low = state.astype(BF16)
            zd = zsum_ref[g]
            kb, vb, qb, nb = spread(k, mask), spread(v, mask), spread(q, mask), spread(dn, mask)
            dden = dot(w, mask)
            line = dot_t(ones, spread(w, mask))[0:1]
            da = jnp.where(lower, dot_t(dn, vb) + dden, 0.0).astype(BF16)
            turned = jnp.where(upper, dot_t(k, qb), 0.0).astype(BF16)
            dat = jnp.where(upper, dot_t(v, nb) + line, 0.0).astype(BF16)
            dq = dot_t(dn, s_ref[g, c]) + dden * z_ref[g, c][0:1] + dot(da, kb)
            dk = dot_t(v, low) + zd[0:1] + dot(dat, qb)
            dv = dot(k, low) + dot(turned, nb)
            dr_ref[0, g, pl.ds(at, BLK), :] = (dq * jnp.minimum(q.astype(F32), 1.0)).astype(BF16)
            dr_ref[1, g, pl.ds(at, BLK), :] = (dk * jnp.minimum(k.astype(F32), 1.0)).astype(BF16)
            dr_ref[2, g, pl.ds(at, BLK), :] = dv.astype(BF16)
            state_ref[g] = state + dot(q.T, dn) * maskf
            zsum_ref[g] = zd + jnp.sum(dden * q.astype(F32), axis=0, keepdims=True)
        return 0

    lax.fori_loop(0, nblk, chunk, 0, unroll=2)

    for g in range(2):
        for j in range(4):
            if j < 3:
                both = dot(h1t_ref[...], dr_ref[j, g]).astype(BF16)
            else:
                both = dot(dmt_ref[...], o_ref[g]).astype(BF16)
            for p in range(2):
                where = (p ^ core) if g == 0 else p
                grad_ref[where, g, :, j * part : (j + 1) * part] = both[:, p * part : (p + 1) * part]

    gain = gain_ref[...]

    def finish(t, _):
        at = pl.multiple_of(t * TILE, TILE)
        dh1 = jnp.zeros((TILE, d), F32)
        for g in range(2):
            for j in range(3):
                w = wown_ref[j] if g == 0 else wg_ref[j]
                dh1 = dh1 + dot_t(dr_ref[j, g, pl.ds(at, TILE), :], w)
        xhat, inv = norm_parts(x_ref[pl.ds(at, TILE), :].astype(F32))
        vec_ref[0:1, :] += jnp.sum(dh1 * xhat, axis=0, keepdims=True)
        vec_ref[1:2, :] += jnp.sum(dh1, axis=0, keepdims=True)
        dx = (dm_ref[pl.ds(at, TILE), :] + norm_back(dh1, xhat, inv, gain)).astype(BF16)
        left, right = dx[:, :half], dx[:, half:]
        first = core == 0
        keep_ref[pl.ds(at, TILE), :] = jnp.where(first, left, right)
        send_ref[pl.ds(at, TILE), :] = jnp.where(first, right, left)
        return 0

    lax.fori_loop(0, seq // TILE, finish, 0)


def return_body(ids_ref, spos_ref, mine_ref, other_ref, out_ref):
    core = ids_ref[0]
    seq = mine_ref.shape[0]

    def step(t, _):
        at = pl.multiple_of(t * TILE, TILE)
        where = spos_ref[pl.ds(at, TILE), :]
        lane = iota((TILE, seq), 1)
        a = dot(one_hot(lane + core * seq == where), mine_ref[...])
        b = dot(one_hot(lane + (1 - core) * seq == where), other_ref[...])
        out_ref[pl.ds(at, TILE), :] = (a + b).astype(BF16)
        return 0

    lax.fori_loop(0, 2 * seq // TILE, step, 0)


def arrive_body(place_ref, mine_ref, other_ref, out_ref):
    rows = out_ref.shape[0]
    seq = rows // 2
    half = mine_ref.shape[3]

    def step(t, _):
        at = pl.multiple_of(t * TILE, TILE)
        where = place_ref[pl.ds(at, TILE), :]
        lane = iota((TILE, seq), 1)
        first = one_hot(lane == where)
        second = one_hot(lane + seq == where)
        for side in range(2):
            a = dot(first, mine_ref[:, side].reshape(seq, half))
            b = dot(second, other_ref[:, side].reshape(seq, half))
            out_ref[pl.ds(at, TILE), side * half : (side + 1) * half] = (a + b).astype(BF16)
        return 0

    lax.fori_loop(0, rows // TILE, step, 0)


def per_device(
    tokens,
    seq_lengths,
    packed_slot,
    out_grad,
    qkv_weight,
    out_weight,
    up_weight,
    down_weight,
    gain_first,
    shift_first,
    gain_second,
    shift_second,
    up_bias,
):
    rows, d = tokens.shape
    count = lax.axis_size("dp")
    slot = rows // count
    half = d // 2
    seq = rows // 2
    nblk = seq // BLK
    width = 4 * HD
    part = width // 2
    unit = up_weight.shape[1] // 2
    device = lax.axis_index("dp")
    core = device % 2
    plane = lax.axis_index("tensor")
    ids = jnp.stack([core, plane]).astype(jnp.int32)
    cores = [(i, i ^ 1) for i in range(count)]
    planes = [(0, 1), (1, 0)]

    def swap_core(x):
        return lax.ppermute(x, "dp", cores)

    def swap_plane(x):
        return lax.ppermute(x, "tensor", planes)

    def trade(x):
        return lax.all_to_all(x, "dp", split_axis=0, concat_axis=0, tiled=True)

    def turn(x):
        return x.reshape(1, -1)

    slots_row = packed_slot.reshape(1, rows)
    tok_send, place = call(
        send_tokens_body,
        (shaped((count, slot + HEADER, half), BF16), shaped((1, rows), jnp.int32)),
        in_specs=[SMEM, VMEM, VMEM],
        flops=rows * rows * d,
        moved=rows * d * 3,
    )(ids, slots_row, tokens)
    tok_mine = trade(tok_send)
    grad_send = call(
        send_grads_body,
        shaped((count, slot, half), BF16),
        in_specs=[VMEM, VMEM],
        flops=rows * rows * d,
        moved=rows * d * 3,
    )(place, out_grad)

    qkv_piece = lax.dynamic_slice_in_dim(qkv_weight, core * part, part, axis=2)
    bias_own = up_bias.reshape(2, unit)
    bias_c = lax.dynamic_slice_in_dim(bias_own, core, 1, axis=0)
    bias_hi = bias_c.astype(BF16)
    left = bias_c - bias_hi.astype(F32)
    bias_mid = left.astype(BF16)
    bias_lo = (left - bias_mid.astype(F32)).astype(BF16)
    ffn_piece = jnp.concatenate(
        [
            lax.dynamic_slice_in_dim(up_weight, core * unit, unit, axis=1),
            lax.dynamic_slice_in_dim(down_weight, core * unit, unit, axis=0),
            lax.dynamic_slice_in_dim(out_weight, core * part, part, axis=0),
            bias_hi,
            bias_mid,
            bias_lo,
            jnp.zeros((13, d), BF16),
        ],
        axis=0,
    )
    qkv_a = swap_plane(qkv_piece)
    qkv_b = swap_core(qkv_a)
    ffn_a = swap_plane(ffn_piece)
    ffn_b = swap_core(ffn_a)

    def unpack(p):
        up = p[:d]
        down = p[d : d + unit]
        out = p[d + unit : d + unit + part]
        at = d + unit + part
        bias = p[at : at + 3].astype(F32)
        return up, down, out, bias[0:1] + bias[1:2] + bias[2:3]

    up_a, down_a, out_a, bias_a = unpack(ffn_a)
    up_b, down_b, out_b, bias_b = unpack(ffn_b)
    bias = jnp.concatenate([bias_own, bias_a, bias_b, jnp.zeros((4, unit), F32)], axis=0)

    tok_other = swap_core(tok_mine)
    off = ((device // 2) % (TILE // slot)) * slot
    marks = lax.dynamic_slice_in_dim(tok_mine[:, slot : slot + 2, :], off, slot, axis=2).astype(F32)
    spos = (marks[:, 0] * 128.0 + marks[:, 1]).astype(jnp.int32)
    spos_row = spos.reshape(1, rows)
    spos_col = spos.reshape(rows, 1)

    x, h1, qkv, o, rden, states, zsums, middle = call(
        attend_body,
        (
            shaped((seq, d), BF16),
            shaped((seq, d), BF16),
            shaped((3, 2, seq, width), BF16),
            shaped((2, seq, width), BF16),
            shaped((2, seq, width), F32),
            shaped((2, nblk, width, width), BF16),
            shaped((2, nblk, 8, width), F32),
            shaped((seq, d), F32),
        ),
        scratch=(
            pltpu.VMEM((3, d, width), BF16),
            pltpu.VMEM((width, d), BF16),
            pltpu.VMEM((2, width, width), F32),
            pltpu.VMEM((2, 8, width), F32),
        ),
        in_specs=[SMEM] + [VMEM] * 11,
        flops=8 * 10**9,
        moved=20 * 10**6,
    )(
        ids, spos_row, tok_mine, tok_other, qkv_weight, qkv_a, qkv_b, out_weight, out_a, out_b,
        turn(gain_first), turn(shift_first),
    )

    grad_mine = trade(grad_send)
    grad_other = swap_core(grad_mine)

    out_keep, out_send, dmiddle, ffn_grads, vec2, bvec = call(
        ffn_body,
        (
            shaped((seq, half), BF16),
            shaped((seq, half), BF16),
            shaped((seq, d), F32),
            shaped((2, 2, 2, d, unit), BF16),
            shaped((8, d), F32),
            shaped((8, unit), F32),
        ),
        scratch=(
            pltpu.VMEM((d, seq), BF16),
            pltpu.VMEM((d, seq), BF16),
            pltpu.VMEM((4, seq, unit), BF16),
            pltpu.VMEM((4, seq, unit), BF16),
        ),
        in_specs=[SMEM] + [VMEM] * 13,
        flops=16 * 10**9,
        moved=20 * 10**6,
    )(
        ids, spos_row, grad_mine, grad_other, middle, up_weight, up_a, up_b,
        down_weight, down_a, down_b, bias, turn(gain_second), turn(shift_second),
    )

    place_col = place.reshape(rows, 1)

    def go_back(keep, send):
        other = swap_core(send)
        ordered = call(
            return_body,
            shaped((rows, half), BF16),
            in_specs=[SMEM, VMEM, VMEM, VMEM],
            flops=rows * rows * d,
            moved=rows * d * 3,
        )(ids, spos_col, keep, other)
        mine = trade(ordered.reshape(count, slot, half))
        far = swap_plane(mine)
        return call(
            arrive_body,
            shaped((rows, d), BF16),
            in_specs=[VMEM, VMEM, VMEM],
            flops=2 * rows * rows * d,
            moved=rows * d * 4,
        )(place_col, mine.reshape(count // 2, 2, slot, half), far.reshape(count // 2, 2, slot, half))

    layer_out = go_back(out_keep, out_send)

    groups = [[c + 2 * k for k in range(count // 2)] for c in range(2)]

    def add(a, b):
        return (a.astype(F32) + b.astype(F32)).astype(BF16)

    def reduce(grads, extra):
        kept, sent = grads[0], grads[1]
        shape = kept.shape[1:]
        kept = kept.reshape(2, -1, d)
        sent = sent.reshape(2, -1, d)
        n = kept.shape[1]
        if extra is not None:
            sent = jnp.concatenate([sent.reshape(2 * n, d), extra], axis=0)
            kept = jnp.concatenate([kept.reshape(2 * n, d), extra], axis=0)
        else:
            sent = sent.reshape(2 * n, d)
            kept = kept.reshape(2 * n, d)
        total = add(kept, swap_core(sent))
        own, far = total[:n], total[n:]
        if extra is not None:
            own = jnp.concatenate([own, total[2 * n :]], axis=0)
        own = add(own, swap_plane(far))
        own = lax.psum(own, "dp", axis_index_groups=groups)
        return own[:n].reshape(shape), (own[n:] if extra is not None else None)

    ffn_sum, _ = reduce(ffn_grads, None)

    in_keep, in_send, attn_grads, vec1 = call(
        attend_back_body,
        (
            shaped((seq, half), BF16),
            shaped((seq, half), BF16),
            shaped((2, 2, d, 4 * part), BF16),
            shaped((8, d), F32),
        ),
        scratch=(
            pltpu.VMEM((3, d, width), BF16),
            pltpu.VMEM((width, d), BF16),
            pltpu.VMEM((d, seq), BF16),
            pltpu.VMEM((d, seq), BF16),
            pltpu.VMEM((2, seq, width), BF16),
            pltpu.VMEM((2, seq, width), BF16),
            pltpu.VMEM((3, 2, seq, width), BF16),
            pltpu.VMEM((2, width, width), F32),
            pltpu.VMEM((2, 8, width), F32),
        ),
        in_specs=[SMEM] + [VMEM] * 15,
        flops=12 * 10**9,
        moved=20 * 10**6,
    )(
        ids, dmiddle, out_weight, out_a, out_b, qkv, o, rden, states, zsums,
        h1, x, qkv_weight, qkv_a, qkv_b, turn(gain_first),
    )
    grad_input = go_back(in_keep, in_send)

    pieces = bvec[:4]
    ours = pieces[:2]
    theirs = jnp.where(core == 0, pieces[2:4], pieces[3:1:-1])
    halves = jnp.where(
        plane == 0,
        jnp.concatenate([ours, theirs], axis=0),
        jnp.concatenate([theirs, ours], axis=0),
    )
    extra = jnp.concatenate(
        [vec1[:2], vec2[:2], halves, jnp.zeros((8, d), F32)], axis=0
    ).astype(BF16)
    attn_sum, vec_sum = reduce(attn_grads, extra)

    def both(mine):
        other = swap_core(mine)
        return jnp.where(core == 0, mine, other), jnp.where(core == 0, other, mine)

    ffn0, ffn1 = both(ffn_sum)
    attn0, attn1 = both(attn_sum)
    grad_up = jnp.concatenate([ffn0[0], ffn1[0]], axis=1).astype(F32)
    grad_down = jnp.concatenate([ffn0[1].T, ffn1[1].T], axis=0).astype(F32)
    grad_qkv = jnp.stack(
        [
            jnp.concatenate([attn0[:, j * part : (j + 1) * part], attn1[:, j * part : (j + 1) * part]], axis=1)
            for j in range(3)
        ]
    ).astype(F32)
    grad_outproj = jnp.concatenate([attn0[:, 3 * part :].T, attn1[:, 3 * part :].T], axis=0).astype(F32)
    vec_sum = vec_sum.astype(F32)
    bias_sum = vec_sum[4:8].reshape(2, 2 * unit)
    grad_up_bias = jnp.where(plane == 0, bias_sum[0], bias_sum[1])
    return (
        layer_out,
        grad_input,
        grad_qkv,
        grad_outproj,
        grad_up,
        grad_down,
        vec_sum[0],
        vec_sum[1],
        vec_sum[2],
        vec_sum[3],
        grad_up_bias,
    )


def solution(mesh):
    placed = (
        P("dp", None),
        P("dp"),
        P("dp"),
        P("dp", None),
        P(None, None, "tensor"),
        P("tensor", None),
        P(None, "tensor"),
        P("tensor", None),
        P(),
        P(),
        P(),
        P(),
        P("tensor"),
    )
    return jax.shard_map(
        per_device,
        mesh=mesh,
        in_specs=placed,
        out_specs=(
            P("dp", None),
            P("dp", None),
            P(None, None, "tensor"),
            P("tensor", None),
            P(None, "tensor"),
            P("tensor", None),
            P(),
            P(),
            P(),
            P(),
            P("tensor"),
        ),
        check_vma=False,
    )
```

```python
import functools

import jax
import jax.numpy as jnp
from jax import lax
from jax.experimental import pallas as pl
from jax.experimental.pallas import tpu as pltpu
from jax.sharding import PartitionSpec as P

HD = 64
BLK = 64
TILE = 256
HEADER = 8
EPS = 1e-05
BF16 = jnp.bfloat16
F32 = jnp.float32
VMEM_LIMIT = 56 * 1024 * 1024


def dot(a, b):
    return jnp.dot(a, b, preferred_element_type=F32)


def dot_t(a, b):
    return lax.dot_general(a, b, (((1,), (1,)), ((), ())), preferred_element_type=F32)


def iota(shape, dim):
    return lax.broadcasted_iota(jnp.int32, shape, dim)


def one_hot(match):
    return jnp.where(match, 1.0, 0.0).astype(BF16)


def call(body, outs, scratch=(), in_specs=None, flops=0, moved=0, trans=0, limit=VMEM_LIMIT):
    return pl.pallas_call(
        body,
        out_shape=outs,
        in_specs=in_specs,
        scratch_shapes=list(scratch),
        compiler_params=pltpu.CompilerParams(vmem_limit_bytes=limit),
        cost_estimate=pl.CostEstimate(flops=flops, bytes_accessed=moved, transcendentals=trans),
    )


def shaped(shape, kind):
    return jax.ShapeDtypeStruct(shape, kind)


SMEM = pl.BlockSpec(memory_space=pltpu.SMEM)
VMEM = pl.BlockSpec(memory_space=pltpu.VMEM)


def send_tokens_body(ids_ref, slot_ref, tok_ref, out_ref, place_ref):
    own_plane = ids_ref[1]
    rows = tok_ref.shape[0]
    count, slot = out_ref.shape[0], out_ref.shape[1] - HEADER
    half = out_ref.shape[2]
    slots = slot_ref[...]
    block = slots // rows
    local = slots - block * rows
    member = one_hot(iota((count, rows), 0) == block)
    before = one_hot(iota((TILE, TILE), 0) < iota((TILE, TILE), 1))
    carry = jnp.zeros((count, 1), F32)
    ranks = []
    for at in range(0, rows, TILE):
        seg = member[:, at : at + TILE]
        inside = dot(seg, before) + carry
        segf = seg.astype(F32)
        ranks.append(jnp.sum(segf * inside, axis=0, keepdims=True))
        carry = carry + jnp.sum(segf, axis=1, keepdims=True)
    rank = jnp.concatenate(ranks, axis=1).astype(jnp.int32)
    pair = block // 2
    place = pair * slot + rank + jnp.where(block - 2 * pair == own_plane, 0, rows // 2)
    place_ref[...] = place
    high = local // 128
    low = local - high * 128
    line = iota((16, rows), 0)
    marks = jnp.where(line == 0, high, jnp.where(line == 1, low, 0)).astype(F32).astype(BF16)
    per = TILE // slot

    def step(t, _):
        pick = one_hot(iota((TILE, rows), 0) + t * TILE == place)
        moved = dot(pick, tok_ref[...]).astype(BF16)
        head = dot_t(marks, pick)[:HEADER].astype(BF16)
        for j in range(per):
            for side in range(2):
                to = 2 * (t * per + j) + side
                out_ref[to, 0:slot, :] = moved[
                    j * slot : (j + 1) * slot, side * half : (side + 1) * half
                ]
                out_ref[to, slot : slot + HEADER, :] = head
        return 0

    lax.fori_loop(0, rows // 2 // TILE, step, 0)


def send_grads_body(place_ref, tok_ref, out_ref):
    rows = tok_ref.shape[0]
    slot, half = out_ref.shape[1], out_ref.shape[2]
    per = TILE // slot
    place = place_ref[...]

    def step(t, _):
        pick = one_hot(iota((TILE, rows), 0) + t * TILE == place)
        moved = dot(pick, tok_ref[...]).astype(BF16)
        for j in range(per):
            for side in range(2):
                out_ref[2 * (t * per + j) + side] = moved[
                    j * slot : (j + 1) * slot, side * half : (side + 1) * half
                ]
        return 0

    lax.fori_loop(0, rows // 2 // TILE, step, 0)


def received(core, pick, mine, other):
    a = dot(pick, mine)
    b = dot(pick, other)
    first = core == 0
    return jnp.concatenate([jnp.where(first, a, b), jnp.where(first, b, a)], axis=1)


def norm_parts(value):
    mean = jnp.mean(value, axis=-1, keepdims=True)
    cent = value - mean
    var = jnp.mean(cent * cent, axis=-1, keepdims=True)
    inv = lax.rsqrt(var + EPS)
    return cent * inv, inv


def norm_back(grad, xhat, inv, gain):
    e = grad * gain
    m1 = jnp.mean(e, axis=-1, keepdims=True)
    m2 = jnp.mean(e * xhat, axis=-1, keepdims=True)
    return inv * (e - m1 - xhat * m2)


def feature(value):
    return jnp.where(value > 0, value + 1.0, jnp.exp(jnp.minimum(value, 0.0)))


def head_mask(kind):
    n = 4 * HD
    return (iota((n, n), 0) // HD == iota((n, n), 1) // HD).astype(F32).astype(kind)


def spread(x, mask):
    return jnp.concatenate([x, x, x, x], axis=0) * mask


def unpack_heads(wa_ref, wb_ref, wg_ref, og_ref):
    part = wa_ref.shape[2]
    for j in range(3):
        wg_ref[j, :, 0:part] = wa_ref[j]
        wg_ref[j, :, part : 2 * part] = wb_ref[j]
    for side, ref in enumerate((wa_ref, wb_ref)):
        for k in range(og_ref.shape[1] // part):
            og_ref[side * part : (side + 1) * part, k * part : (k + 1) * part] = ref[
                3, k * part : (k + 1) * part, :
            ]


def attend_body(
    ids_ref, spos_ref, mine_ref, other_ref, wown_ref, wa_ref, wb_ref, oown_ref,
    gain_ref, shift_ref,
    x_ref, h1_ref, qkv_ref, o_ref, rden_ref, s_ref, z_ref, m_ref,
    wg_ref, og_ref, state_ref, zsum_ref,
):
    core = ids_ref[0]
    count, slot, half = mine_ref.shape[0], mine_ref.shape[1] - HEADER, mine_ref.shape[2]
    rows = count * slot
    seq = rows // 2
    width = 4 * HD
    unpack_heads(wa_ref, wb_ref, wg_ref, og_ref)
    spos = spos_ref[...]
    gain, shift = gain_ref[...], shift_ref[...]

    def project(t, _):
        at = pl.multiple_of(t * TILE, TILE)
        pick = one_hot(iota((TILE, rows), 0) + core * seq + t * TILE == spos)
        mine = mine_ref[:, 0:slot, :].reshape(rows, half)
        other = other_ref[:, 0:slot, :].reshape(rows, half)
        x = received(core, pick, mine, other)
        x_ref[pl.ds(at, TILE), :] = x.astype(BF16)
        xhat, _inv = norm_parts(x)
        h1 = (xhat * gain + shift).astype(BF16)
        h1_ref[pl.ds(at, TILE), :] = h1
        for g in range(2):
            for j in range(3):
                w = wown_ref[j] if g == 0 else wg_ref[j]
                u = dot(h1, w)
                if j < 2:
                    u = feature(u)
                qkv_ref[j, g, pl.ds(at, TILE), :] = u.astype(BF16)
        return 0

    lax.fori_loop(0, seq // TILE, project, 0)

    state_ref[...] = jnp.zeros_like(state_ref)
    zsum_ref[...] = jnp.zeros_like(zsum_ref)
    maskf = head_mask(F32)
    mask = maskf.astype(BF16)
    lower = iota((BLK, width), 1) % BLK <= iota((BLK, width), 0)

    def chunk(c, _):
        at = pl.multiple_of(c * BLK, BLK)
        for g in range(2):
            q = qkv_ref[0, g, pl.ds(at, BLK), :]
            k = qkv_ref[1, g, pl.ds(at, BLK), :]
            v = qkv_ref[2, g, pl.ds(at, BLK), :]
            state = state_ref[g]
            low = state.astype(BF16)
            s_ref[g, c] = low
            z = zsum_ref[g]
            z_ref[g, c] = z
            scores = jnp.where(lower, dot_t(q, spread(k, mask)), 0.0)
            num = dot(q, low) + dot(scores.astype(BF16), spread(v, mask))
            den = dot((scores + q.astype(F32) * z[0:1]).astype(BF16), mask) + 1e-06
            rden = 1.0 / den
            rden_ref[g, pl.ds(at, BLK), :] = rden
            o_ref[g, pl.ds(at, BLK), :] = (num * rden).astype(BF16)
            state_ref[g] = state + dot(k.T, v) * maskf
            zsum_ref[g] = z + jnp.sum(k.astype(F32), axis=0, keepdims=True)
        return 0

    lax.fori_loop(0, seq // BLK, chunk, 0, unroll=2)

    def output(t, _):
        at = pl.multiple_of(t * TILE, TILE)
        att = dot(o_ref[0, pl.ds(at, TILE), :], oown_ref[...])
        att = att + dot(o_ref[1, pl.ds(at, TILE), :], og_ref[...])
        m_ref[pl.ds(at, TILE), :] = x_ref[pl.ds(at, TILE), :].astype(F32) + att
        return 0

    lax.fori_loop(0, seq // TILE, output, 0)


def ffn_body(
    ids_ref, spos_ref, mine_ref, other_ref, m_ref, uown_ref, ua_ref, ub_ref,
    down_ref, da_ref, db_ref, bias_ref, gain_ref, shift_ref,
    keep_ref, send_ref, dm_ref, gkeep_ref, gsend_ref, vec_ref, bvec_ref,
    gpt_ref, h2t_ref, rl_ref, du_ref,
):
    core = ids_ref[0]
    count, slot, half = mine_ref.shape
    rows = count * slot
    seq = rows // 2
    d, unit = m_ref.shape[1], ua_ref.shape[1]
    spos = spos_ref[...]
    gain, shift = gain_ref[...], shift_ref[...]
    vec_ref[...] = jnp.zeros_like(vec_ref)
    bvec_ref[...] = jnp.zeros_like(bvec_ref)

    far = []
    for ref in (ua_ref, ub_ref):
        three = ref[d : d + 16, :].astype(F32)
        far.append(three[0:1] + three[1:2] + three[2:3])

    def bias_piece(j):
        return bias_ref[j : j + 1, :] if j < 2 else far[j - 2]

    def up_piece(j):
        if j < 2:
            return uown_ref[:, j * unit : (j + 1) * unit]
        return ua_ref[0:d, :] if j == 2 else ub_ref[0:d, :]

    def down_piece(j):
        if j < 2:
            return down_ref[j * unit : (j + 1) * unit, :]
        return da_ref[...] if j == 2 else db_ref[...]

    def tile(t, _):
        at = pl.multiple_of(t * TILE, TILE)
        pick = one_hot(iota((TILE, rows), 0) + core * seq + t * TILE == spos)
        gpf = received(core, pick, mine_ref[...].reshape(rows, half), other_ref[...].reshape(rows, half))
        gp = gpf.astype(BF16)
        m = m_ref[pl.ds(at, TILE), :]
        xhat, inv = norm_parts(m)
        h2 = (xhat * gain + shift).astype(BF16)
        gpt_ref[:, pl.ds(at, TILE)] = gp.T
        h2t_ref[:, pl.ds(at, TILE)] = h2.T
        f = jnp.zeros((TILE, m.shape[1]), F32)
        dh2 = jnp.zeros((TILE, m.shape[1]), F32)
        for j in range(4):
            up, down = up_piece(j), down_piece(j)
            u = dot(h2, up) + bias_piece(j)
            sig = jax.nn.sigmoid(u)
            rl = (u * sig).astype(BF16)
            rl_ref[j, pl.ds(at, TILE), :] = rl
            f = f + dot(rl, down)
            du = dot_t(gp, down) * (sig * (1.0 + u * (1.0 - sig)))
            dul = du.astype(BF16)
            du_ref[j, pl.ds(at, TILE), :] = dul
            bvec_ref[j : j + 1, :] += jnp.sum(dul.astype(F32), axis=0, keepdims=True)
            dh2 = dh2 + dot_t(dul, up)
        out = (m + f).astype(BF16)
        left, right = out[:, :half], out[:, half:]
        first = core == 0
        keep_ref[pl.ds(at, TILE), :] = jnp.where(first, left, right)
        send_ref[pl.ds(at, TILE), :] = jnp.where(first, right, left)
        vec_ref[0:1, :] += jnp.sum(dh2 * xhat, axis=0, keepdims=True)
        vec_ref[1:2, :] += jnp.sum(dh2, axis=0, keepdims=True)
        dm_ref[pl.ds(at, TILE), :] = gpf + norm_back(dh2, xhat, inv, gain)
        return 0

    lax.fori_loop(0, seq // TILE, tile, 0)

    for to_ref, side, j in ((gsend_ref, 1, 3), (gkeep_ref, 1, 2), (gsend_ref, 0, 1 - core), (gkeep_ref, 0, core)):
        to_ref[0, side] = dot(h2t_ref[...], du_ref[j]).astype(BF16)
        to_ref[1, side] = dot(gpt_ref[...], rl_ref[j]).astype(BF16)


def attend_back_body(
    ids_ref, dm_ref, oown_ref, qkv_ref, o_ref, rden_ref, s_ref, z_ref,
    h1_ref, x_ref, wown_ref, wa_ref, wb_ref, gain_ref, vec2_ref, bvec_ref,
    keep_ref, send_ref, gkeep_ref, gsend_ref,
    wg_ref, og_ref, dmt_ref, h1t_ref, dn_ref, w_ref, dr_ref, state_ref, zsum_ref, vec_ref,
):
    core = ids_ref[0]
    seq, d = dm_ref.shape
    width = 4 * HD
    part = width // 2
    half = keep_ref.shape[1]
    lines = gkeep_ref.shape[2]
    cut = min(d, lines)
    unpack_heads(wa_ref, wb_ref, wg_ref, og_ref)
    vec_ref[...] = jnp.zeros_like(vec_ref)

    def start(t, _):
        at = pl.multiple_of(t * TILE, TILE)
        dml = dm_ref[pl.ds(at, TILE), :].astype(BF16)
        dmt_ref[:, pl.ds(at, TILE)] = dml.T
        h1t_ref[:, pl.ds(at, TILE)] = h1_ref[pl.ds(at, TILE), :].T
        for g in range(2):
            do = dot_t(dml, oown_ref[...] if g == 0 else og_ref[...])
            dn = do * rden_ref[g, pl.ds(at, TILE), :]
            dn_ref[g, pl.ds(at, TILE), :] = dn.astype(BF16)
            w_ref[g, pl.ds(at, TILE), :] = (
                -dn * o_ref[g, pl.ds(at, TILE), :].astype(F32)
            ).astype(BF16)
        return 0

    lax.fori_loop(0, seq // TILE, start, 0)

    state_ref[...] = jnp.zeros_like(state_ref)
    zsum_ref[...] = jnp.zeros_like(zsum_ref)
    maskf = head_mask(F32)
    mask = maskf.astype(BF16)
    ones = jnp.ones((16, width), BF16)
    lower = iota((BLK, width), 1) % BLK <= iota((BLK, width), 0)
    upper = iota((BLK, width), 1) % BLK >= iota((BLK, width), 0)
    nblk = seq // BLK

    def chunk(step, _):
        c = nblk - 1 - step
        at = pl.multiple_of(c * BLK, BLK)
        for g in range(2):
            q = qkv_ref[0, g, pl.ds(at, BLK), :]
            k = qkv_ref[1, g, pl.ds(at, BLK), :]
            v = qkv_ref[2, g, pl.ds(at, BLK), :]
            dn = dn_ref[g, pl.ds(at, BLK), :]
            w = w_ref[g, pl.ds(at, BLK), :]
            state = state_ref[g]
            low = state.astype(BF16)
            zd = zsum_ref[g]
            kb, vb, qb, nb = spread(k, mask), spread(v, mask), spread(q, mask), spread(dn, mask)
            dden = dot(w, mask)
            line = dot_t(ones, spread(w, mask))[0:1]
            da = jnp.where(lower, dot_t(dn, vb) + dden, 0.0).astype(BF16)
            turned = jnp.where(upper, dot_t(k, qb), 0.0).astype(BF16)
            dat = jnp.where(upper, dot_t(v, nb) + line, 0.0).astype(BF16)
            dq = dot_t(dn, s_ref[g, c]) + dden * z_ref[g, c][0:1] + dot(da, kb)
            dk = dot_t(v, low) + zd[0:1] + dot(dat, qb)
            dv = dot(k, low) + dot(turned, nb)
            dr_ref[0, g, pl.ds(at, BLK), :] = (dq * jnp.minimum(q.astype(F32), 1.0)).astype(BF16)
            dr_ref[1, g, pl.ds(at, BLK), :] = (dk * jnp.minimum(k.astype(F32), 1.0)).astype(BF16)
            dr_ref[2, g, pl.ds(at, BLK), :] = dv.astype(BF16)
            state_ref[g] = state + dot(q.T, dn) * maskf
            zsum_ref[g] = zd + jnp.sum(dden * q.astype(F32), axis=0, keepdims=True)
        return 0

    lax.fori_loop(0, nblk, chunk, 0, unroll=2)

    for g in range(2):
        for j in range(4):
            if j < 3:
                both = dot(h1t_ref[...], dr_ref[j, g]).astype(BF16)
            else:
                both = dot(dmt_ref[...], o_ref[g]).astype(BF16)
            left, right = both[:, :part], both[:, part:]
            first = core == 0
            kept = jnp.where(first, left, right) if g == 0 else left
            sent = jnp.where(first, right, left) if g == 0 else right
            for to_ref, value in ((gkeep_ref, kept), (gsend_ref, sent)):
                lanes = slice(j * part, (j + 1) * part)
                to_ref[0, g, 0:cut, lanes] = value[0:cut]
                if cut < d:
                    to_ref[1, g, 0 : d - cut, lanes] = value[cut:d]

    gain = gain_ref[...]

    def finish(t, _):
        at = pl.multiple_of(t * TILE, TILE)
        dh1 = jnp.zeros((TILE, d), F32)
        for g in range(2):
            for j in range(3):
                w = wown_ref[j] if g == 0 else wg_ref[j]
                dh1 = dh1 + dot_t(dr_ref[j, g, pl.ds(at, TILE), :], w)
        xhat, inv = norm_parts(x_ref[pl.ds(at, TILE), :].astype(F32))
        vec_ref[0:1, :] += jnp.sum(dh1 * xhat, axis=0, keepdims=True)
        vec_ref[1:2, :] += jnp.sum(dh1, axis=0, keepdims=True)
        dx = (dm_ref[pl.ds(at, TILE), :] + norm_back(dh1, xhat, inv, gain)).astype(BF16)
        left, right = dx[:, :half], dx[:, half:]
        first = core == 0
        keep_ref[pl.ds(at, TILE), :] = jnp.where(first, left, right)
        send_ref[pl.ds(at, TILE), :] = jnp.where(first, right, left)
        return 0

    lax.fori_loop(0, seq // TILE, finish, 0)

    plane = ids_ref[1]
    row = iota((16, d), 0)
    block = jnp.zeros((16, d), F32)
    for line, value in enumerate((vec_ref[0:1, :], vec_ref[1:2, :], vec2_ref[0:1, :], vec2_ref[1:2, :])):
        block = jnp.where(row == line, value, block)
    for j in range(4):
        at = 4 + 2 * plane + j if j < 2 else 6 - 2 * plane + (core if j == 2 else 1 - core)
        block = jnp.where(row == at, bvec_ref[j : j + 1, :], block)
    low = block.astype(BF16)
    for ref in (gkeep_ref, gsend_ref):
        for g in range(2):
            if lines > d - cut + 16:
                ref[1, g, d - cut + 16 :, :] = jnp.zeros((lines - d + cut - 16, d), BF16)
            ref[1, g, d - cut : d - cut + 16, :] = low


def return_body(ids_ref, spos_ref, mine_ref, other_ref, out_ref):
    core = ids_ref[0]
    seq = mine_ref.shape[0]

    def step(t, _):
        at = pl.multiple_of(t * TILE, TILE)
        where = spos_ref[pl.ds(at, TILE), :]
        lane = iota((TILE, seq), 1)
        a = dot(one_hot(lane + core * seq == where), mine_ref[...])
        b = dot(one_hot(lane + (1 - core) * seq == where), other_ref[...])
        out_ref[pl.ds(at, TILE), :] = (a + b).astype(BF16)
        return 0

    lax.fori_loop(0, 2 * seq // TILE, step, 0)


def arrive_body(far, place_ref, mine_ref, *refs):
    out_ref = refs[-1]
    rows = out_ref.shape[0]
    seq = rows // 2
    half = mine_ref.shape[3]

    def step(t, _):
        at = pl.multiple_of(t * TILE, TILE)
        where = place_ref[pl.ds(at, TILE), :]
        pick = one_hot(iota((TILE, seq), 1) + far * seq == where)
        for side in range(2):
            a = dot(pick, mine_ref[:, side].reshape(seq, half))
            if far:
                a = a + refs[0][pl.ds(at, TILE), side * half : (side + 1) * half].astype(F32)
            out_ref[pl.ds(at, TILE), side * half : (side + 1) * half] = a.astype(BF16)
        return 0

    lax.fori_loop(0, rows // TILE, step, 0)


def chunks_of(ref, bits, to_ref):
    n, size = ref.shape[0], ref.shape[1]
    for k in range(n):
        to_ref[k * size : (k + 1) * size, :] = ref[k ^ bits]


def ffn_grads_body(ids_ref, mine_ref, other_ref, up_ref, down_ref, a_ref, b_ref):
    core, bits = ids_ref[0], ids_ref[2]
    d, unit = up_ref.shape[0], down_ref.shape[1]
    unit = up_ref.shape[1] // 2
    chunks_of(mine_ref, bits, a_ref)
    chunks_of(other_ref, bits, b_ref)
    first = core == 0
    for p in range(2):
        take = first if p == 0 else jnp.logical_not(first)
        up = jnp.where(take, a_ref[0:d, :], b_ref[0:d, :])
        down = jnp.where(take, a_ref[d : 2 * d, :], b_ref[d : 2 * d, :])
        up_ref[:, p * unit : (p + 1) * unit] = up.astype(F32)
        down_ref[p * unit : (p + 1) * unit, :] = down.T.astype(F32)


def attn_grads_body(ids_ref, mine_ref, other_ref, qkv_ref, out_ref, vec_ref, a_ref, b_ref):
    core, bits = ids_ref[0], ids_ref[2]
    d, part = qkv_ref.shape[1], qkv_ref.shape[2] // 2
    chunks_of(mine_ref, bits, a_ref)
    chunks_of(other_ref, bits, b_ref)
    first = core == 0
    for p in range(2):
        take = first if p == 0 else jnp.logical_not(first)
        both = jnp.where(take, a_ref[0:d, :], b_ref[0:d, :])
        for j in range(3):
            qkv_ref[j, :, p * part : (p + 1) * part] = both[:, j * part : (j + 1) * part].astype(F32)
        out_ref[p * part : (p + 1) * part, :] = both[:, 3 * part : 4 * part].T.astype(F32)
    vec_ref[...] = a_ref[d : d + 16, :].astype(F32)


def per_device(
    tokens,
    seq_lengths,
    packed_slot,
    out_grad,
    qkv_weight,
    out_weight,
    up_weight,
    down_weight,
    gain_first,
    shift_first,
    gain_second,
    shift_second,
    up_bias,
):
    rows, d = tokens.shape
    count = lax.axis_size("dp")
    slot = rows // count
    half = d // 2
    seq = rows // 2
    nblk = seq // BLK
    width = 4 * HD
    part = width // 2
    unit = up_weight.shape[1] // 2
    device = lax.axis_index("dp")
    core = device % 2
    plane = lax.axis_index("tensor")
    levels = [1 << b for b in range(1, count.bit_length() - 1)]
    bits = 0
    for bit in levels:
        bits = 2 * bits + (device // bit) % 2
    ids = jnp.stack([core, plane, bits]).astype(jnp.int32)
    planes = [(0, 1), (1, 0)]

    def across(x, bit):
        return lax.ppermute(x, "dp", [(i, i ^ bit) for i in range(count)])

    def swap_core(x):
        return across(x, 1)

    def swap_plane(x):
        return lax.ppermute(x, "tensor", planes)

    def trade(x):
        return lax.all_to_all(x, "dp", split_axis=0, concat_axis=0, tiled=True)

    def turn(x):
        return x.reshape(1, -1)

    def after(x, *deps):
        return lax.optimization_barrier((x, *deps))[0]

    slots_row = packed_slot.reshape(1, rows)
    tok_send, place = call(
        send_tokens_body,
        (shaped((count, slot + HEADER, half), BF16), shaped((1, rows), jnp.int32)),
        in_specs=[SMEM, VMEM, VMEM],
        flops=rows * rows * d,
        moved=rows * d * 3,
    )(ids, slots_row, tokens)
    tok_mine = trade(tok_send)

    def piece(x, size, axis):
        return lax.dynamic_slice_in_dim(x, core * size, size, axis=axis)

    qkv_weight_late, out_weight_late, up_late, down_late, bias_late = lax.optimization_barrier(
        (qkv_weight, out_weight, up_weight, down_weight, up_bias, tok_send)
    )[:5]
    out_piece = piece(out_weight_late, part, 0).reshape(part, d // part, part)
    out_piece = jnp.transpose(out_piece, (1, 0, 2)).reshape(1, d, part)
    heads_a = swap_plane(jnp.concatenate([piece(qkv_weight_late, part, 2), out_piece], axis=0))
    bias_own = up_bias.reshape(2, unit)
    bias_c = piece(bias_late.reshape(2, unit), 1, 0)
    bias_hi = bias_c.astype(BF16)
    left = bias_c - bias_hi.astype(F32)
    bias_mid = left.astype(BF16)
    bias_lo = (left - bias_mid.astype(F32)).astype(BF16)
    up_piece = jnp.concatenate(
        [piece(up_late, unit, 1), bias_hi, bias_mid, bias_lo, jnp.zeros((13, unit), BF16)], axis=0
    )
    up_a = swap_plane(up_piece)
    down_piece = piece(down_late, unit, 0)
    down_a = swap_plane(down_piece)

    grad_send = call(
        send_grads_body,
        shaped((count, slot, half), BF16),
        in_specs=[VMEM, VMEM],
        flops=rows * rows * d,
        moved=rows * d * 3,
    )(after(place, heads_a, up_piece, down_piece), out_grad)
    heads_b = swap_core(heads_a)
    place_col = place.reshape(rows, 1)

    tok_mine = after(tok_mine, grad_send)
    tok_other = swap_core(tok_mine)
    grad_mine = trade(after(grad_send, tok_mine))
    up_b = swap_core(up_a)
    down_b = swap_core(down_a)
    off = ((device // 2) % (TILE // slot)) * slot
    marks = lax.dynamic_slice_in_dim(tok_mine[:, slot : slot + 2, :], off, slot, axis=2).astype(F32)
    spos = (marks[:, 0] * 128.0 + marks[:, 1]).astype(jnp.int32)
    spos_row = spos.reshape(1, rows)
    spos_col = spos.reshape(rows, 1)

    x, h1, qkv, o, rden, states, zsums, middle = call(
        attend_body,
        (
            shaped((seq, d), BF16),
            shaped((seq, d), BF16),
            shaped((3, 2, seq, width), BF16),
            shaped((2, seq, width), BF16),
            shaped((2, seq, width), F32),
            shaped((2, nblk, width, width), BF16),
            shaped((2, nblk, 8, width), F32),
            shaped((seq, d), F32),
        ),
        scratch=(
            pltpu.VMEM((3, d, width), BF16),
            pltpu.VMEM((width, d), BF16),
            pltpu.VMEM((2, width, width), F32),
            pltpu.VMEM((2, 8, width), F32),
        ),
        in_specs=[SMEM] + [VMEM] * 9,
        flops=25 * 10**9,
        moved=20 * 10**6,
    )(
        ids, spos_row, tok_mine, tok_other, qkv_weight, heads_a, heads_b, out_weight,
        turn(gain_first), turn(shift_first),
    )

    grad_mine = after(grad_mine, middle)
    grad_other = swap_core(grad_mine)
    grad_kind = shaped((2, 2, d, unit), BF16)

    out_keep, out_send, dmiddle, f_keep, f_send, vec2, bvec = call(
        ffn_body,
        (
            shaped((seq, half), BF16),
            shaped((seq, half), BF16),
            shaped((seq, d), F32),
            grad_kind,
            grad_kind,
            shaped((8, d), F32),
            shaped((8, unit), F32),
        ),
        scratch=(
            pltpu.VMEM((d, seq), BF16),
            pltpu.VMEM((d, seq), BF16),
            pltpu.VMEM((4, seq, unit), BF16),
            pltpu.VMEM((4, seq, unit), BF16),
        ),
        in_specs=[SMEM] + [VMEM] * 13,
        flops=25 * 10**9,
        moved=20 * 10**6,
    )(
        ids, spos_row, grad_mine, grad_other, middle, up_weight, up_a, up_b,
        down_weight, down_a, down_b, bias_own, turn(gain_second), turn(shift_second),
    )

    def order(keep, send):
        other = swap_core(send)
        return call(
            return_body,
            shaped((rows, half), BF16),
            in_specs=[SMEM, VMEM, VMEM, VMEM],
            flops=rows * rows * d,
            moved=rows * d * 3,
        )(ids, spos_col, keep, other).reshape(count, slot, half)

    def arrive(mine):
        far = swap_plane(mine)
        shape = (count // 2, 2, slot, half)
        near = call(
            functools.partial(arrive_body, 0),
            shaped((rows, d), BF16),
            in_specs=[VMEM, VMEM],
            flops=rows * rows * d,
            moved=rows * d * 4,
        )(place_col, mine.reshape(shape))
        return call(
            functools.partial(arrive_body, 1),
            shaped((rows, d), BF16),
            in_specs=[VMEM, VMEM, VMEM],
            flops=rows * rows * d,
            moved=rows * d * 4,
        )(place_col, far.reshape(shape), near)

    def add(a, b):
        return (a.astype(F32) + b.astype(F32)).astype(BF16)

    def sides(x, bit):
        high = (device // bit) % 2
        return (
            lax.dynamic_index_in_dim(x, high, 0, keepdims=False),
            lax.dynamic_index_in_dim(x, 1 - high, 0, keepdims=False),
        )

    def reduce_near(x):
        kept, sent = sides(x, levels[0])
        return add(kept, across(sent, levels[0]))

    def reduce_rest(x):
        for bit in levels[1:]:
            kept, sent = sides(x.reshape(2, x.shape[0] // 2, x.shape[1]), bit)
            x = add(kept, across(sent, bit))
        for bit in reversed(levels):
            x = jnp.concatenate([x, across(x, bit)], axis=0)
        return x

    ordered = order(out_keep, out_send)
    out_mine = trade(ordered)
    f_total = add(f_keep, swap_core(f_send))
    f_near = reduce_near(f_total)

    size = 8 * (count // 2)
    lines = -(-(d + 16) // size) * size
    piece_kind = shaped((2, 2, lines // 2, 4 * part), BF16)
    in_keep, in_send, a_keep, a_send = call(
        attend_back_body,
        (
            shaped((seq, half), BF16),
            shaped((seq, half), BF16),
            piece_kind,
            piece_kind,
        ),
        scratch=(
            pltpu.VMEM((3, d, width), BF16),
            pltpu.VMEM((width, d), BF16),
            pltpu.VMEM((d, seq), BF16),
            pltpu.VMEM((d, seq), BF16),
            pltpu.VMEM((2, seq, width), BF16),
            pltpu.VMEM((2, seq, width), BF16),
            pltpu.VMEM((3, 2, seq, width), BF16),
            pltpu.VMEM((2, width, width), F32),
            pltpu.VMEM((2, 8, width), F32),
            pltpu.VMEM((8, d), F32),
        ),
        in_specs=[SMEM] + [VMEM] * 15,
        flops=25 * 10**9,
        moved=20 * 10**6,
    )(
        ids, after(dmiddle, ordered, f_total), out_weight, qkv, o, rden, states, zsums,
        h1, x, qkv_weight, heads_a, heads_b, turn(gain_first), vec2, bvec,
    )
    in_ordered = order(after(in_keep, out_mine, f_near), in_send)
    in_mine = trade(in_ordered)
    f_sum = reduce_rest(add(f_near[0], swap_plane(f_near[1])))
    a_total = add(after(a_keep, in_ordered), swap_core(a_send))
    a_near = reduce_near(a_total)
    a_sum = reduce_rest(add(a_near[0], swap_plane(a_near[1])))

    groups = count // 2
    f_sum = f_sum.reshape(groups, -1, unit)
    grad_up, grad_down = call(
        ffn_grads_body,
        (shaped((d, 2 * unit), F32), shaped((2 * unit, d), F32)),
        scratch=(pltpu.VMEM((2 * d, unit), BF16), pltpu.VMEM((2 * d, unit), BF16)),
        in_specs=[SMEM, VMEM, VMEM],
        flops=10**9,
        moved=6 * 10**6,
    )(ids, f_sum, swap_core(f_sum))
    a_sum = a_sum.reshape(groups, -1, 4 * part)
    grad_qkv, grad_outproj, vec_sum = call(
        attn_grads_body,
        (shaped((3, d, width), F32), shaped((width, d), F32), shaped((16, d), F32)),
        scratch=(pltpu.VMEM((lines, 4 * part), BF16), pltpu.VMEM((lines, 4 * part), BF16)),
        in_specs=[SMEM, VMEM, VMEM],
        flops=10**9,
        moved=4 * 10**6,
    )(ids, a_sum, swap_core(a_sum))
    bias_sum = vec_sum[4:8].reshape(2, 2 * unit)
    grad_up_bias = jnp.where(plane == 0, bias_sum[0], bias_sum[1])

    layer_out = arrive(out_mine)
    grad_input = arrive(in_mine)
    return (
        layer_out,
        grad_input,
        grad_qkv,
        grad_outproj,
        grad_up,
        grad_down,
        vec_sum[0],
        vec_sum[1],
        vec_sum[2],
        vec_sum[3],
        grad_up_bias,
    )


def solution(mesh):
    placed = (
        P("dp", None),
        P("dp"),
        P("dp"),
        P("dp", None),
        P(None, None, "tensor"),
        P("tensor", None),
        P(None, "tensor"),
        P("tensor", None),
        P(),
        P(),
        P(),
        P(),
        P("tensor"),
    )
    return jax.shard_map(
        per_device,
        mesh=mesh,
        in_specs=placed,
        out_specs=(
            P("dp", None),
            P("dp", None),
            P(None, None, "tensor"),
            P("tensor", None),
            P(None, "tensor"),
            P("tensor", None),
            P(),
            P(),
            P(),
            P(),
            P("tensor"),
        ),
        check_vma=False,
    )
```
